256 devices in a mesh: dp: 8 (over x, core), context: 32 (over y, z).
Axes of the slice: x: 4, y: 4, z: 8, core: 2. Of those that a mesh axis runs over, the one named last changes fastest.
Arguments:
- queries: bfloat16 [32768, 4096], P(('dp', 'context')), may hold values from -8 to 8
- keys: bfloat16 [32768, 512], P(('dp', 'context')), may hold values from -8 to 8
- tokens: bfloat16 [32768, 4096], P(('dp', 'context')), may hold values from -24 to 24
- value_matrix: bfloat16 [4096, 512], P(('dp', 'context')), may hold values from -0.09375 to 0.09375
- output_gradient: bfloat16 [32768, 4096], P(('dp', 'context')), may hold values from -6 to 6
- segment_lengths: int32 [8, 64], P('dp'), may hold values from 1 to 128, 4096 in all within a row
- segment_offsets: int32 [8, 64], P('dp'), may hold values from 0 to 64
Outputs:
- dqueries: bfloat16 [32768, 4096], P(('dp', 'context'))
- dkeys: bfloat16 [32768, 512], P(('dp', 'context'))
- dtokens: bfloat16 [32768, 4096], P(('dp', 'context'))
- dweight: float32 [4096, 512], P(('dp', 'context'))
The draws below stay inside these ranges and needn't reach their ends.
Inputs may be any that keep to these rules, and one draw needn't show every extreme that they name: `segment_lengths`: each row holds the lengths of one sequence's 64 segments, in order, summing to 4096.
All inputs are finite; a program needn't handle non-finite values.
Results may differ from the reference program's by a relative error of at most 0.015.
Values may be sent and summed in bfloat16 or wider, within the bound.
No kernel may reach another device: no remote copies, remote signals or barrier semaphores. Data moves between devices by JAX's collectives and lax.ppermute only.
A program may use at most 128 MiB of HBM per device.

```python
import math
import jax
import jax.numpy as jnp
import numpy as np
from jax import lax

MODEL_WIDTH = 4096
QUERY_HEADS = 32
KEY_VALUE_HEADS = 4
HEAD_SIZE = 128
SEG = 128
PACKED_LENGTH = 4096
NSEG = 64
TOKEN_TOTAL = 32768
N_DP = 8


def drawn_pair(key):
    base_offset = jax.random.fold_in(key, 11)
    queries_out = jnp.clip(jax.random.normal(jax.random.fold_in(base_offset, 1), (TOKEN_TOTAL, QUERY_HEADS * HEAD_SIZE), jnp.float32), -6.0, 6.0)
    key_output = jnp.clip(jax.random.normal(jax.random.fold_in(base_offset, 2), (TOKEN_TOTAL, KEY_VALUE_HEADS * HEAD_SIZE), jnp.float32), -6.0, 6.0)
    return (queries_out, key_output)


def draw_queries(key, part):
    return drawn_pair(key)[0].astype(jnp.bfloat16)


def draw_keys(key, part):
    return drawn_pair(key)[1].astype(jnp.bfloat16)


def plant(values, key, smallest, top_value):
    dims = values.shape
    place = [jax.random.randint(jax.random.fold_in(key, axis), (), 0, dims[axis]) for axis in range(len(dims))]
    values = values.at[tuple(place)].set(smallest)
    longest = dims.index(max(dims))
    place[longest] = (place[longest] + 1) % dims[longest]
    return values.at[tuple(place)].set(top_value)


def strengthened(drawn, key, source, target, parts, factor):
    owner, partner = [(jnp.arange(drawn.shape[axis_at]) // (drawn.shape[axis_at] // parts)).reshape([-1 if axis == axis_at else 1 for axis in range(drawn.ndim)]) for axis_at in (source, target)]
    chosen = jax.random.permutation(key, parts)[partner]
    strong = (owner == chosen) | (owner == (partner + parts // 2) % parts)
    return jnp.where(strong, factor * drawn, drawn)


def steps_of(key, dims, cuts, least, largest):
    gain = 1.0
    for position, parts in cuts:
        steps = jax.random.uniform(jax.random.fold_in(jax.random.fold_in(key, 6), position), (parts,), jnp.float32, least / len(cuts), largest / len(cuts))
        gain = gain * jnp.repeat(jnp.exp(steps), dims[position] // parts).reshape((-1,) + (1,) * (len(dims) - 1 - position))
    return gain


def split_up(count, total, most, lean):
    portions = [(1 << 20) // math.isqrt(standing ** lean) + 1 for standing in range(2, count + 1)]
    surplus, given = total - most - (count - 1), [1] * (count - 1)
    while surplus > 0:
        movable = [i for i in range(count - 1) if given[i] < most]
        whole, budget = sum([portions[i] for i in movable]), surplus
        for i in movable:
            addition = min(most - given[i], max(1, budget * portions[i] // whole), surplus)
            given[i] = given[i] + addition
            surplus = surplus - addition
    return np.array([most] + given)


def ragged_sizes(own_key, amount, total, limit, slope):
    if amount == 2:
        one = jax.random.randint(own_key, (), max(1, total - limit), min(limit, total - 1) + 1)
        return jnp.stack([one, total - one])
    lengths = jnp.asarray(split_up(amount, total, limit, slope), jnp.int32)
    pairs = (amount - 1) // 2
    source_of, receiver = lengths[1:1 + 2 * pairs:2], lengths[2:2 + 2 * pairs:2]
    slack = jnp.minimum(source_of - 1, limit - receiver)
    passed = jax.random.randint(jax.random.fold_in(own_key, 1), (pairs,), 0, 1 << 20) % (slack + 1)
    lengths = lengths.at[1:1 + 2 * pairs:2].set(source_of - passed).at[2:2 + 2 * pairs:2].set(receiver + passed)
    return lengths[jax.random.permutation(jax.random.fold_in(own_key, 2), amount)]


def normal_values(rng, extent, scale, limit, pieces=(), kind=jnp.bfloat16):
    loudness = steps_of(rng, extent, pieces, -0.22, 0.18) if pieces else 1.0
    entries = jax.random.normal(rng, extent, jnp.float32) * scale * loudness
    return jnp.minimum(jnp.maximum(entries, -limit), limit).astype(kind)


def noise_with(own_key, shape, spread, most, shards, heavy, kind=jnp.bfloat16):
    entries = spread * jax.random.normal(own_key, shape, jnp.float32)
    if shards:
        entries = entries * steps_of(own_key, shape, shards, -0.22, 0.18)
    return jnp.clip(strengthened(entries, jax.random.fold_in(own_key, 3), *heavy), -most, most).astype(kind)


def setup_inputs(seed: int = 0) -> dict:
    key_list = jax.random.split(jax.random.key(seed), 8)
    queries = draw_queries(jax.random.fold_in(key_list[7], 71), 0)
    keys = draw_keys(jax.random.fold_in(key_list[7], 71), 0)
    tokens = noise_with(key_list[2], (TOKEN_TOTAL, MODEL_WIDTH), 1.0, 24.0, ((0, 256),), (0, 1, 256, 6.0))
    value_matrix = normal_values(key_list[3], (MODEL_WIDTH, KEY_VALUE_HEADS * HEAD_SIZE), MODEL_WIDTH ** -0.5, 0.09375, ((0, 256),))
    output_gradient = normal_values(key_list[4], (TOKEN_TOTAL, QUERY_HEADS * HEAD_SIZE), 1.0, 6.0, ((0, 256),))
    segment_lengths = jax.vmap(lambda own: ragged_sizes(own, NSEG, PACKED_LENGTH, SEG, 2))(jax.random.split(key_list[5], N_DP)).reshape((N_DP, NSEG)).astype(jnp.int32)
    segment_offsets = plant(jax.random.randint(key_list[6], (N_DP, NSEG), 0, SEG // 2 + 1), jax.random.fold_in(key_list[6], 1), 0, (SEG // 2 + 1) - 1).astype(jnp.int32)
    return dict(queries=queries, keys=keys, tokens=tokens, value_matrix=value_matrix, output_gradient=output_gradient, segment_lengths=segment_lengths, segment_offsets=segment_offsets)


def segment_info(positions, lengths_row, offsets_row):
    ends = jnp.cumsum(lengths_row).astype(jnp.int32)
    starts = (ends - lengths_row).astype(jnp.int32)
    prefix = jnp.minimum(offsets_row, lengths_row).astype(jnp.int32)
    inside = (positions >= 0) & (positions < PACKED_LENGTH)
    segment = lax.optimization_barrier(jnp.sum((ends[None, :] <= positions[:, None]).astype(jnp.int32), axis=1)).astype(jnp.int32)
    onehot = segment[:, None] == jnp.arange(lengths_row.shape[0], dtype=jnp.int32)[None, :]
    start = lax.optimization_barrier(jnp.sum(jnp.where(onehot, starts[None, :], 0), axis=1)).astype(jnp.int32)
    reach = start + lax.optimization_barrier(jnp.sum(jnp.where(onehot, prefix[None, :], 0), axis=1)).astype(jnp.int32)
    segment = jnp.where(inside, segment, -1).astype(jnp.int32)
    return (segment, reach)

def visible_mask(query_pos, key_pos, lengths_row, offsets_row):
    query_seg, query_reach = segment_info(query_pos, lengths_row, offsets_row)
    key_seg, unused = segment_info(key_pos, lengths_row, offsets_row)
    same = query_seg[:, None] == key_seg[None, :]
    before = key_pos[None, :] <= query_pos[:, None]
    prefix = key_pos[None, :] < query_reach[:, None]
    return same & (before | prefix)

def block_grads(query, keys, value_tensor, output_gradient, visible):
    scale = 1.0 / math.sqrt(HEAD_SIZE)
    query_f = query.astype(jnp.float32)
    keys_f = keys.astype(jnp.float32)
    values_f = value_tensor.astype(jnp.float32)
    grad_f = output_gradient.astype(jnp.float32)
    scores = jnp.einsum('rkgd,ckd->kgrc', query_f, keys_f) * scale
    scores = jnp.where(visible[None, None], scores, -jnp.inf)
    top = lax.optimization_barrier(jnp.max(scores, axis=-1, keepdims=True))
    weights = jnp.exp(scores - top)
    probs = weights / lax.optimization_barrier(jnp.sum(weights, axis=-1, keepdims=True))
    dprobs = jnp.einsum('rkgd,ckd->kgrc', grad_f, values_f)
    delta = lax.optimization_barrier(jnp.sum(probs * dprobs, axis=-1, keepdims=True))
    dscores = (probs * (dprobs - delta) * scale).astype(jnp.bfloat16)
    probs_low = probs.astype(jnp.bfloat16)
    dscores = lax.optimization_barrier(dscores).astype(jnp.float32)
    probs_low = lax.optimization_barrier(probs_low).astype(jnp.float32)
    query_gradient = jnp.einsum('kgrc,ckd->rkgd', dscores, keys_f)
    dkeys = jnp.einsum('kgrc,rkgd->ckgd', dscores, query_f)
    value_gradient = jnp.einsum('kgrc,rkgd->ckgd', probs_low, grad_f)
    return (query_gradient, dkeys, value_gradient)

def one_group(items):
    query, keys, value_tensor, output_gradient, lengths_row, offsets_row = items
    query_group = query.shape[1]
    rows = min(256, PACKED_LENGTH)
    count = PACKED_LENGTH // rows
    width = rows + 2 * SEG
    pad_keys = jnp.pad(keys, ((SEG, SEG), (0, 0)))
    pad_values = jnp.pad(value_tensor, ((SEG, SEG), (0, 0)))

    def step(carry, index):
        dkeys_acc, dvalues_acc = carry
        first = (index * rows).astype(jnp.int32)
        query_pos = first + jnp.arange(rows, dtype=jnp.int32)
        key_pos = first - SEG + jnp.arange(width, dtype=jnp.int32)
        visible = visible_mask(query_pos, key_pos, lengths_row, offsets_row)
        query_block = lax.dynamic_slice_in_dim(query, first, rows, 0)[:, None]
        grad_block = lax.dynamic_slice_in_dim(output_gradient, first, rows, 0)[:, None]
        keys_block = lax.dynamic_slice_in_dim(pad_keys, first, width, 0)[:, None]
        values_block = lax.dynamic_slice_in_dim(pad_values, first, width, 0)[:, None]
        query_gradient, dkeys, value_gradient = block_grads(query_block, keys_block, values_block, grad_block, visible)
        dkeys_acc = lax.dynamic_update_slice_in_dim(dkeys_acc, lax.dynamic_slice_in_dim(dkeys_acc, first, width, 0) + lax.optimization_barrier(jnp.sum(dkeys[:, 0], axis=1)), first, 0)
        dvalues_acc = lax.dynamic_update_slice_in_dim(dvalues_acc, lax.dynamic_slice_in_dim(dvalues_acc, first, width, 0) + lax.optimization_barrier(jnp.sum(value_gradient[:, 0], axis=1)), first, 0)
        return ((dkeys_acc, dvalues_acc), query_gradient[:, 0])
    zeros = jnp.zeros((PACKED_LENGTH + 2 * SEG, HEAD_SIZE), jnp.float32)
    (dkeys_acc, dvalues_acc), dquery_blocks = lax.scan(step, (zeros, zeros), jnp.arange(count, dtype=jnp.int32))
    query_gradient = dquery_blocks.reshape(PACKED_LENGTH, query_group, HEAD_SIZE).astype(jnp.bfloat16)
    dkeys = dkeys_acc[SEG:SEG + PACKED_LENGTH].astype(jnp.bfloat16)
    value_gradient = dvalues_acc[SEG:SEG + PACKED_LENGTH].astype(jnp.bfloat16)
    return (query_gradient, dkeys, value_gradient)

def reference(queries, keys, tokens, value_matrix, output_gradient, segment_lengths, segment_offsets):
    query_group = QUERY_HEADS // KEY_VALUE_HEADS
    value_tensor = jnp.dot(tokens, value_matrix, preferred_element_type=jnp.float32).astype(jnp.bfloat16)
    query_rows_all = queries.reshape(N_DP, PACKED_LENGTH, KEY_VALUE_HEADS, query_group, HEAD_SIZE).transpose(0, 2, 1, 3, 4).reshape(N_DP * KEY_VALUE_HEADS, PACKED_LENGTH, query_group, HEAD_SIZE)
    gradient_rows_all = output_gradient.reshape(N_DP, PACKED_LENGTH, KEY_VALUE_HEADS, query_group, HEAD_SIZE).transpose(0, 2, 1, 3, 4).reshape(N_DP * KEY_VALUE_HEADS, PACKED_LENGTH, query_group, HEAD_SIZE)
    key_rows_all = keys.reshape(N_DP, PACKED_LENGTH, KEY_VALUE_HEADS, HEAD_SIZE).transpose(0, 2, 1, 3).reshape(N_DP * KEY_VALUE_HEADS, PACKED_LENGTH, HEAD_SIZE)
    value_rows_all = value_tensor.reshape(N_DP, PACKED_LENGTH, KEY_VALUE_HEADS, HEAD_SIZE).transpose(0, 2, 1, 3).reshape(N_DP * KEY_VALUE_HEADS, PACKED_LENGTH, HEAD_SIZE)
    segment_lengths_all = jnp.repeat(segment_lengths, KEY_VALUE_HEADS, axis=0)
    segment_offsets_all = jnp.repeat(segment_offsets, KEY_VALUE_HEADS, axis=0)
    query_gradient, dkeys, value_gradient = lax.map(one_group, (query_rows_all, key_rows_all, value_rows_all, gradient_rows_all, segment_lengths_all, segment_offsets_all))
    dqueries = query_gradient.reshape(N_DP, KEY_VALUE_HEADS, PACKED_LENGTH, query_group, HEAD_SIZE).transpose(0, 2, 1, 3, 4).reshape(N_DP * PACKED_LENGTH, QUERY_HEADS * HEAD_SIZE)
    key_gradient_output = dkeys.reshape(N_DP, KEY_VALUE_HEADS, PACKED_LENGTH, HEAD_SIZE).transpose(0, 2, 1, 3).reshape(N_DP * PACKED_LENGTH, KEY_VALUE_HEADS * HEAD_SIZE)
    value_gradient_output = value_gradient.reshape(N_DP, KEY_VALUE_HEADS, PACKED_LENGTH, HEAD_SIZE).transpose(0, 2, 1, 3).reshape(N_DP * PACKED_LENGTH, KEY_VALUE_HEADS * HEAD_SIZE)
    dtokens = jnp.dot(value_gradient_output, value_matrix.T, preferred_element_type=jnp.float32).astype(jnp.bfloat16)
    dweight = jnp.dot(tokens.T, value_gradient_output, preferred_element_type=jnp.float32)
    return (dqueries, key_gradient_output, dtokens, dweight)
```

```python
import math

import jax
import jax.numpy as jnp
from jax import lax
from jax.experimental import pallas as pl
from jax.experimental.pallas import tpu as pltpu
from jax.sharding import PartitionSpec as P

HEAD = 128
LEFT = 128
RIGHT = 64
GROUP = 8
NEG = -1e30

BF = jnp.bfloat16
F32 = jnp.float32


def dot(a, b, ca, cb):
    return lax.dot_general(a, b, (((ca,), (cb,)), ((), ())), preferred_element_type=F32)


def visible_bias(first, rows, lengths, offsets):
    slots = lengths.shape[0]
    order = jnp.arange(slots, dtype=jnp.int32)
    ends = jnp.sum(jnp.where(order[None, :] <= order[:, None], lengths[None, :], 0), axis=1)
    starts = ends - lengths
    prefix = jnp.minimum(offsets, lengths)
    position = first + jnp.arange(rows, dtype=jnp.int32)
    ended = ends[:, None] <= position[None, :]
    begun = starts[:, None] <= position[None, :]
    low = jnp.sum(jnp.where(ended, lengths[:, None], 0), axis=0)
    reach = low + jnp.sum(jnp.where(begun & ~ended, prefix[:, None], 0), axis=0)
    high = jnp.maximum(position + 1, reach)
    key = first - LEFT + jnp.arange(LEFT + rows + RIGHT, dtype=jnp.int32)
    seen = (key[:, None] >= low[None, :]) & (key[:, None] < high[None, :])
    return jnp.where(seen, 0.0, NEG).astype(F32)


def stacked(ref, h):
    return jnp.concatenate([ref[:, h * HEAD : (h + 1) * HEAD], ref[:, (h + 1) * HEAD : (h + 2) * HEAD]], axis=0)


def probs_kernel(q_ref, kl_ref, ko_ref, kr_ref, g_ref, bias_ref, dvl_ref, dvo_ref, dvr_ref, lse_ref):
    scale = 1.0 / math.sqrt(HEAD)
    rows = ko_ref.shape[0]
    k = jnp.concatenate([kl_ref[...], ko_ref[...], kr_ref[...]], axis=0)
    bias = jnp.concatenate([bias_ref[...], bias_ref[...]], axis=1)
    total = None
    for h in range(0, GROUP, 2):
        scores = dot(k, stacked(q_ref, h), 1, 1) * scale + bias
        top = jnp.max(scores, axis=0, keepdims=True)
        weights = jnp.exp(scores - top)
        norm = jnp.sum(weights, axis=0, keepdims=True)
        probs = (weights * (1.0 / norm)).astype(BF)
        lse_ref[0, :, h * HEAD : (h + 2) * HEAD] = top + jnp.log(norm)
        part = dot(probs, stacked(g_ref, h), 1, 0)
        total = part if total is None else total + part
    dvl_ref[...] = total[:LEFT].astype(BF)
    dvo_ref[...] = total[LEFT : LEFT + rows]
    dvr_ref[...] = total[LEFT + rows :].astype(BF)


def scores_kernel(q_ref, kl_ref, ko_ref, kr_ref, vl_ref, vo_ref, vr_ref, g_ref, bias_ref, lse_ref, dq_ref, dkl_ref, dko_ref, dkr_ref):
    scale = 1.0 / math.sqrt(HEAD)
    rows = ko_ref.shape[0]
    k = jnp.concatenate([kl_ref[...], ko_ref[...], kr_ref[...]], axis=0)
    v = jnp.concatenate([vl_ref[...], vo_ref[...], vr_ref[...]], axis=0)
    bias = jnp.concatenate([bias_ref[...], bias_ref[...]], axis=1)
    total = None
    for h in range(0, GROUP, 2):
        q = stacked(q_ref, h)
        scores = dot(k, q, 1, 1) * scale + bias
        probs = jnp.exp(scores - lse_ref[0, :, h * HEAD : (h + 2) * HEAD])
        dprobs = dot(v, stacked(g_ref, h), 1, 1)
        delta = jnp.sum(probs * dprobs, axis=0, keepdims=True)
        dscores = (probs * (dprobs - delta) * scale).astype(BF)
        part = dot(dscores, q, 1, 0)
        total = part if total is None else total + part
        dq = dot(dscores, k, 0, 0).astype(BF)
        dq_ref[:, h * HEAD : (h + 1) * HEAD] = dq[:rows]
        dq_ref[:, (h + 1) * HEAD : (h + 2) * HEAD] = dq[rows:]
    dkl_ref[...] = total[:LEFT].astype(BF)
    dko_ref[...] = total[LEFT : LEFT + rows]
    dkr_ref[...] = total[LEFT + rows :].astype(BF)


def head_spec(rows):
    return pl.BlockSpec((rows, HEAD), lambda g: (0, g))


def wide_spec(rows):
    return pl.BlockSpec((rows, GROUP * HEAD), lambda g: (0, g))


def part_shapes(rows, width):
    return [
        jax.ShapeDtypeStruct((LEFT, width), BF),
        jax.ShapeDtypeStruct((rows, width), F32),
        jax.ShapeDtypeStruct((RIGHT, width), BF),
    ]


def window_specs(rows):
    return [head_spec(LEFT), head_spec(rows), head_spec(RIGHT)]


def attention_probs(q, k, g, bias):
    rows, width = k[1].shape
    heads = width // HEAD
    span = bias.shape[0]
    lse_spec = pl.BlockSpec((1, 1, GROUP * rows), lambda g: (g, 0, 0))
    return pl.pallas_call(
        probs_kernel,
        grid=(heads,),
        in_specs=[wide_spec(rows), *window_specs(rows), wide_spec(rows), pl.BlockSpec((span, rows), lambda g: (0, 0))],
        out_specs=[*window_specs(rows), lse_spec],
        out_shape=[*part_shapes(rows, width), jax.ShapeDtypeStruct((heads, 1, GROUP * rows), F32)],
        compiler_params=pltpu.CompilerParams(dimension_semantics=("arbitrary",), vmem_limit_bytes=40 << 20),
        cost_estimate=pl.CostEstimate(flops=4 * heads * GROUP * rows * span * HEAD, bytes_accessed=3 << 20, transcendentals=heads * GROUP * rows * span),
        name="probs",
    )(q, *k, g, bias)


def attention_scores(q, k, v, g, bias, lse):
    rows, width = k[1].shape
    heads = width // HEAD
    span = bias.shape[0]
    lse_spec = pl.BlockSpec((1, 1, GROUP * rows), lambda g: (g, 0, 0))
    return pl.pallas_call(
        scores_kernel,
        grid=(heads,),
        in_specs=[
            wide_spec(rows),
            *window_specs(rows),
            *window_specs(rows),
            wide_spec(rows),
            pl.BlockSpec((span, rows), lambda g: (0, 0)),
            lse_spec,
        ],
        out_specs=[wide_spec(rows), *window_specs(rows)],
        out_shape=[jax.ShapeDtypeStruct(q.shape, BF), *part_shapes(rows, width)],
        compiler_params=pltpu.CompilerParams(dimension_semantics=("arbitrary",), vmem_limit_bytes=40 << 20),
        cost_estimate=pl.CostEstimate(flops=8 * heads * GROUP * rows * span * HEAD, bytes_accessed=4 << 20, transcendentals=heads * GROUP * rows * span),
        name="scores",
    )(q, *k, *v, g, bias, lse)


def to_right(x):
    count = lax.axis_size("context")
    return lax.ppermute(x, "context", [(i, i + 1) for i in range(count - 1)])


def to_left(x):
    count = lax.axis_size("context")
    return lax.ppermute(x, "context", [(i + 1, i) for i in range(count - 1)])


def windowed(x):
    return (to_right(x[x.shape[0] - LEFT :]), x, to_left(x[:RIGHT]))


def collected(left, own, right):
    rows = own.shape[0]
    from_next = to_left(left)
    from_last = to_right(right)
    total = own + jnp.pad(from_last.astype(F32), ((0, rows - RIGHT), (0, 0)))
    return (total + jnp.pad(from_next.astype(F32), ((rows - LEFT, 0), (0, 0)))).astype(BF)


def gathered(x, axis):
    count = lax.axis_size(axis)
    copies = jnp.broadcast_to(x[None], (count,) + x.shape)
    return lax.all_to_all(copies, axis, 0, 0, tiled=True).reshape(count * x.shape[0], x.shape[1])


def summed(x, axis):
    count = lax.axis_size(axis)
    parts = lax.all_to_all(x.reshape(count, x.shape[0] // count, x.shape[1]), axis, 0, 0, tiled=True)
    return jnp.sum(parts.astype(F32), axis=0)


def shards(queries, keys, tokens, value_matrix, output_gradient, segment_lengths, segment_offsets):
    rows = queries.shape[0]
    first = lax.axis_index("context") * rows
    bias = visible_bias(first, rows, segment_lengths[0], segment_offsets[0])
    k = windowed(keys)
    token_columns = lax.all_to_all(tokens, "dp", 1, 0, tiled=True)
    weight_rows = gathered(value_matrix, "context")
    dv_left, dv_own, dv_right, lse = attention_probs(queries, k, output_gradient, bias)
    dvalues = collected(dv_left, dv_own, dv_right)
    values = summed(dot(token_columns, weight_rows, 1, 0).astype(BF), "dp").astype(BF)
    v = windowed(values)
    all_dvalues = gathered(dvalues, "dp")
    dweight = summed(dot(token_columns, all_dvalues, 0, 0).astype(BF), "context")
    dtokens = lax.all_to_all(dot(all_dvalues, weight_rows, 1, 1).astype(BF), "dp", 0, 1, tiled=True)
    dqueries, dk_left, dk_own, dk_right = attention_scores(queries, k, v, output_gradient, bias, lse)
    dkeys = collected(dk_left, dk_own, dk_right)
    return (dqueries, dkeys, dtokens, dweight)


def solution(mesh):
    both = P(("dp", "context"), None)
    in_specs = (both, both, both, both, both, P("dp", None), P("dp", None))
    out_specs = (both, both, both, both)
    return jax.shard_map(shards, mesh=mesh, in_specs=in_specs, out_specs=out_specs, check_vma=False)
```

```python
import math

import jax
import jax.numpy as jnp
from jax import lax
from jax.experimental import pallas as pl
from jax.experimental.pallas import tpu as pltpu
from jax.sharding import PartitionSpec as P

HEAD = 128
LEFT = 128
RIGHT = 64
GROUP = 8
NEG = -1e30
X_CHIPS = 4

BF = jnp.bfloat16
F32 = jnp.float32


def lasting(us):
    return pl.CostEstimate(flops=int(us * 1.1e9), bytes_accessed=1 << 20, transcendentals=0)


def dot(a, b, ca, cb):
    return lax.dot_general(a, b, (((ca,), (cb,)), ((), ())), preferred_element_type=F32)


def visible_bias(first, rows, lengths, offsets):
    slots = lengths.shape[0]
    order = jnp.arange(slots, dtype=jnp.int32)
    ends = jnp.sum(jnp.where(order[None, :] <= order[:, None], lengths[None, :], 0), axis=1)
    starts = ends - lengths
    prefix = jnp.minimum(offsets, lengths)
    position = first + jnp.arange(rows, dtype=jnp.int32)
    ended = ends[:, None] <= position[None, :]
    begun = starts[:, None] <= position[None, :]
    low = jnp.sum(jnp.where(ended, lengths[:, None], 0), axis=0)
    reach = low + jnp.sum(jnp.where(begun & ~ended, prefix[:, None], 0), axis=0)
    high = jnp.maximum(position + 1, reach)
    key = first - LEFT + jnp.arange(LEFT + rows + RIGHT, dtype=jnp.int32)
    seen = (key[:, None] >= low[None, :]) & (key[:, None] < high[None, :])
    return jnp.where(seen, 0.0, NEG).astype(F32)


def stacked(ref):
    return jnp.concatenate([ref[:, h * HEAD : (h + 1) * HEAD] for h in range(GROUP)], axis=0)


def window(odd, even_pair, own, odd_pair):
    left = jnp.where(odd, even_pair[...], odd_pair[...])
    right = jnp.where(odd, odd_pair[...], even_pair[...])
    return jnp.concatenate([left, own[...], right[:RIGHT]], axis=0)


def scatter_window(odd, total, even_pair, own, odd_pair):
    rows = own.shape[0]
    left = total[:LEFT].astype(BF)
    right = total[LEFT + rows :].astype(BF)
    right = jnp.concatenate([right, jnp.zeros((LEFT - RIGHT, right.shape[1]), BF)], axis=0)
    even_pair[...] = jnp.where(odd, left, right)
    own[...] = total[LEFT : LEFT + rows]
    odd_pair[...] = jnp.where(odd, right, left)


def probs_kernel(where_ref, q_ref, ka_ref, ko_ref, kb_ref, g_ref, bias_ref, dva_ref, dvo_ref, dvb_ref, lse_ref):
    scale = 1.0 / math.sqrt(HEAD)
    odd = where_ref[2] % 2 == 1
    k = window(odd, ka_ref, ko_ref, kb_ref)
    bias = jnp.concatenate([bias_ref[...]] * GROUP, axis=1)
    scores = dot(k, stacked(q_ref), 1, 1) * scale + bias
    top = jnp.max(scores, axis=0, keepdims=True)
    weights = jnp.exp(scores - top)
    norm = jnp.sum(weights, axis=0, keepdims=True)
    probs = (weights * (1.0 / norm)).astype(BF)
    lse_ref[0] = top + jnp.log(norm)
    scatter_window(odd, dot(probs, stacked(g_ref), 1, 0), dva_ref, dvo_ref, dvb_ref)


def scores_kernel(where_ref, q_ref, ka_ref, ko_ref, kb_ref, va_ref, vo_ref, vb_ref, g_ref, bias_ref, lse_ref, dq_ref, dka_ref, dko_ref, dkb_ref):
    scale = 1.0 / math.sqrt(HEAD)
    rows = ko_ref.shape[0]
    odd = where_ref[2] % 2 == 1
    k = window(odd, ka_ref, ko_ref, kb_ref)
    v = window(odd, va_ref, vo_ref, vb_ref)
    bias = jnp.concatenate([bias_ref[...]] * GROUP, axis=1)
    q = stacked(q_ref)
    probs = jnp.exp(dot(k, q, 1, 1) * scale + bias - lse_ref[0])
    dprobs = dot(v, stacked(g_ref), 1, 1)
    delta = jnp.sum(probs * dprobs, axis=0, keepdims=True)
    dscores = (probs * (dprobs - delta) * scale).astype(BF)
    dq = dot(dscores, k, 0, 0).astype(BF)
    for h in range(GROUP):
        dq_ref[:, h * HEAD : (h + 1) * HEAD] = dq[h * rows : (h + 1) * rows]
    scatter_window(odd, dot(dscores, q, 1, 0), dka_ref, dko_ref, dkb_ref)


def head_spec(rows):
    return pl.BlockSpec((rows, HEAD), lambda g, where: (0, g))


def wide_spec(rows):
    return pl.BlockSpec((rows, GROUP * HEAD), lambda g, where: (0, g))


def lse_spec(rows):
    return pl.BlockSpec((1, 1, GROUP * rows), lambda g, where: (g, 0, 0))


def part_shapes(rows, width):
    pair = jax.ShapeDtypeStruct((LEFT, width), BF)
    return [pair, jax.ShapeDtypeStruct((rows, width), F32), pair]


def window_specs(rows):
    return [head_spec(LEFT), head_spec(rows), head_spec(LEFT)]


def attention_probs(where, q, k, g, bias):
    rows, width = k[1].shape
    heads = width // HEAD
    span = bias.shape[0]
    spec = pltpu.PrefetchScalarGridSpec(
        num_scalar_prefetch=1,
        grid=(heads,),
        in_specs=[wide_spec(rows), *window_specs(rows), wide_spec(rows), pl.BlockSpec((span, rows), lambda g, where: (0, 0))],
        out_specs=[*window_specs(rows), lse_spec(rows)],
    )
    return pl.pallas_call(
        probs_kernel,
        grid_spec=spec,
        out_shape=[*part_shapes(rows, width), jax.ShapeDtypeStruct((heads, 1, GROUP * rows), F32)],
        compiler_params=pltpu.CompilerParams(dimension_semantics=("arbitrary",)),
        cost_estimate=lasting(6),
        name="probs",
    )(where, q, *k, g, bias)


def attention_scores(where, q, k, v, g, bias, lse):
    rows, width = k[1].shape
    heads = width // HEAD
    span = bias.shape[0]
    spec = pltpu.PrefetchScalarGridSpec(
        num_scalar_prefetch=1,
        grid=(heads,),
        in_specs=[
            wide_spec(rows),
            *window_specs(rows),
            *window_specs(rows),
            wide_spec(rows),
            pl.BlockSpec((span, rows), lambda g, where: (0, 0)),
            lse_spec(rows),
        ],
        out_specs=[wide_spec(rows), *window_specs(rows)],
    )
    return pl.pallas_call(
        scores_kernel,
        grid_spec=spec,
        out_shape=[jax.ShapeDtypeStruct(q.shape, BF), *part_shapes(rows, width)],
        compiler_params=pltpu.CompilerParams(dimension_semantics=("arbitrary",)),
        cost_estimate=lasting(25),
        name="scores",
    )(where, q, *k, *v, g, bias, lse)


def swapped(x, axis, bits):
    count = lax.axis_size(axis)
    return lax.ppermute(x, axis, [(i, i ^ bits) for i in range(count)])


def pair_swapped(even_pair, odd_pair):
    count = lax.axis_size("context")
    others = [(i, i + 1) for i in range(1, count - 1, 2)]
    others = others + [(b, a) for a, b in others]
    return swapped(even_pair, "context", 1), lax.ppermute(odd_pair, "context", others)


def neighbours(x):
    even_pair, odd_pair = pair_swapped(x, x)
    return (even_pair, x, odd_pair)


def collected(even_pair, own, odd_pair):
    even_pair, odd_pair = pair_swapped(even_pair, odd_pair)
    return (own + even_pair.astype(F32) + odd_pair.astype(F32)).astype(BF)


def split_kernel(where_ref, t1_ref, t2_ref, t3_ref, s1_ref, s2_ref, s3_ref):
    s1_ref[...] = t1_ref[...]
    s2_ref[...] = t2_ref[...]
    s3_ref[...] = t3_ref[...]


def column_spec(rows, width, i):
    return pl.BlockSpec((rows, width), lambda step, where: (0, where[0] ^ i))


def column_blocks(where, tokens):
    rows, width = tokens.shape
    width = width // X_CHIPS
    spec = pltpu.PrefetchScalarGridSpec(
        num_scalar_prefetch=1,
        grid=(1,),
        in_specs=[column_spec(rows, width, i) for i in (1, 2, 3)],
        out_specs=[pl.BlockSpec((rows, width), lambda step, where: (0, 0))] * 3,
    )
    return pl.pallas_call(
        split_kernel,
        grid_spec=spec,
        out_shape=[jax.ShapeDtypeStruct((rows, width), BF)] * 3,
        cost_estimate=lasting(1.5),
        name="split",
    )(where, tokens, tokens, tokens)


def project_kernel(where_ref, t0_ref, t1_ref, t2_ref, t3_ref, mine_ref, theirs_ref, part_ref, acc_ref):
    step = pl.program_id(0)
    tokens = jnp.concatenate([t0_ref[...], t1_ref[...], t2_ref[...], t3_ref[...]], axis=0)

    @pl.when(step == 0)
    def _():
        acc_ref[...] = dot(tokens, mine_ref[...], 1, 0)

    @pl.when(step == 1)
    def _():
        part = (acc_ref[...] + dot(tokens, theirs_ref[...], 1, 0)).astype(BF)
        rows = part_ref.shape[1]
        for i in range(X_CHIPS):
            part_ref[where_ref[0] ^ i] = part[i * rows : (i + 1) * rows]


def half_specs(rows, depth):
    own = pl.BlockSpec((rows, depth), lambda step, where: (0, where[0] * 2 + (where[1] ^ step)))
    other = pl.BlockSpec((rows, depth), lambda step, where: (0, where[1] ^ step))
    return [own] + [other] * 3


def projected(where, tokens, columns, mine, theirs):
    rows = tokens.shape[0]
    depth, width = mine.shape
    whole = pl.BlockSpec((depth, width), lambda step, where: (0, 0))
    spec = pltpu.PrefetchScalarGridSpec(
        num_scalar_prefetch=1,
        grid=(2,),
        in_specs=half_specs(rows, depth) + [whole, whole],
        out_specs=pl.BlockSpec((X_CHIPS, rows, width), lambda step, where: (0, 0, 0)),
        scratch_shapes=[pltpu.VMEM((X_CHIPS * rows, width), F32)],
    )
    return pl.pallas_call(
        project_kernel,
        grid_spec=spec,
        out_shape=jax.ShapeDtypeStruct((X_CHIPS, rows, width), BF),
        compiler_params=pltpu.CompilerParams(dimension_semantics=("arbitrary",)),
        cost_estimate=lasting(4),
        name="project",
    )(where, tokens, *columns, mine, theirs)


def weight_kernel(where_ref, t0_ref, t1_ref, t2_ref, t3_ref, d0_ref, d1_ref, d2_ref, d3_ref, mine_ref, theirs_ref, send_ref, keep_ref, *back_refs):
    step = pl.program_id(0)
    tokens = jnp.concatenate([t0_ref[...], t1_ref[...], t2_ref[...], t3_ref[...]], axis=0)
    dvalues = jnp.concatenate([d0_ref[...], d1_ref[...], d2_ref[...], d3_ref[...]], axis=0)
    part = dot(tokens, dvalues, 0, 0)
    rows = d0_ref.shape[0]

    @pl.when(step == 0)
    def _():
        send_ref[...] = part.astype(BF)
        back = dot(dvalues, theirs_ref[...], 1, 1).astype(BF)
        for i, ref in enumerate(back_refs):
            ref[...] = back[i * rows : (i + 1) * rows]

    @pl.when(step == 1)
    def _():
        keep_ref[...] = part
        back = dot(dvalues, mine_ref[...], 1, 1).astype(BF)
        for i, ref in enumerate(back_refs):
            ref[...] = back[i * rows : (i + 1) * rows]


def weight_partials(where, tokens, columns, dvalues, mine, theirs):
    rows = tokens.shape[0]
    depth, width = mine.shape
    whole = pl.BlockSpec((depth, width), lambda step, where: (0, 0))
    part = pl.BlockSpec((rows, width), lambda step, where: (0, 0))
    own = pl.BlockSpec((rows, depth), lambda step, where: (0, where[0] * 2 + (1 - (where[1] ^ step))))
    other = pl.BlockSpec((rows, depth), lambda step, where: (0, 1 - (where[1] ^ step)))
    spec = pltpu.PrefetchScalarGridSpec(
        num_scalar_prefetch=1,
        grid=(2,),
        in_specs=[own] + [other] * 3 + [part] * 4 + [whole, whole],
        out_specs=[whole, whole] + [other] * 4,
    )
    return pl.pallas_call(
        weight_kernel,
        grid_spec=spec,
        out_shape=[jax.ShapeDtypeStruct((depth, width), BF), jax.ShapeDtypeStruct((depth, width), F32)]
        + [jax.ShapeDtypeStruct((rows, 2 * depth), BF)] * 4,
        compiler_params=pltpu.CompilerParams(dimension_semantics=("arbitrary",)),
        cost_estimate=lasting(5),
        name="weights",
    )(where, tokens, *columns, *dvalues, mine, theirs)


def place_kernel(where_ref, t0_ref, t1_ref, t2_ref, t3_ref, out_ref):
    width = t0_ref.shape[1]
    for i, ref in enumerate((t0_ref, t1_ref, t2_ref, t3_ref)):
        at = pl.multiple_of((where_ref[0] ^ i) * width, width)
        out_ref[:, pl.ds(at, width)] = ref[...]


def placed(where, pieces):
    rows, width = pieces[0].shape
    return pl.pallas_call(
        place_kernel,
        in_specs=[pl.BlockSpec(memory_space=pltpu.SMEM)] + [pl.BlockSpec(memory_space=pltpu.VMEM)] * 4,
        out_specs=pl.BlockSpec(memory_space=pltpu.VMEM),
        out_shape=jax.ShapeDtypeStruct((rows, X_CHIPS * width), BF),
        cost_estimate=lasting(2.4),
        name="place",
    )(where, *pieces)


def after(earlier, *later):
    return lax.optimization_barrier((later, earlier))[0]


def shards(queries, keys, tokens, value_matrix, output_gradient, segment_lengths, segment_offsets):
    rows = queries.shape[0]
    place = lax.axis_index("context")
    dp = lax.axis_index("dp")
    contexts = lax.axis_size("context")
    where = jnp.stack([dp // 2, dp % 2, place]).astype(jnp.int32)
    bias = visible_bias(place * rows, rows, segment_lengths[0], segment_offsets[0])

    copies = jnp.broadcast_to(value_matrix[None], (contexts,) + value_matrix.shape)
    mine = lax.all_to_all(copies, "context", 0, 0, tiled=True)
    mine = mine.reshape(contexts * value_matrix.shape[0], value_matrix.shape[1])
    theirs = swapped(mine, "dp", 1)
    (moving_tokens,) = after(copies, tokens)
    sent = column_blocks(where, moving_tokens)
    columns = [swapped(sent[i - 1], "dp", 2 * i) for i in (1, 2, 3)]
    (moving_keys,) = after(sent, keys)
    k_even, unused, k_odd = neighbours(moving_keys)
    k = (k_even, keys, k_odd)
    (bias,) = after((columns, mine), bias)

    dv_even, dv_own, dv_odd, lse = attention_probs(where, queries, k, output_gradient, bias)
    dvalues = collected(dv_even, dv_own, dv_odd)
    all_dvalues = [dvalues] + [swapped(dvalues, "dp", 2 * i) for i in (1, 2, 3)]

    groups = [[2 * x + core for x in range(X_CHIPS)] for core in range(2)]
    started = projected(where, tokens, columns, mine, theirs)
    parts = lax.all_to_all(started, "dp", 0, 0, axis_index_groups=groups, tiled=True)
    values = jnp.sum(parts.astype(F32), axis=0).astype(BF)
    v = neighbours(values)

    all_dvalues = after(started, *all_dvalues)
    send, keep, *back = weight_partials(where, tokens, columns, all_dvalues, mine, theirs)
    share = (keep + swapped(send, "dp", 1).astype(F32)).astype(BF)
    share = share.reshape(contexts, -1, share.shape[1])
    dweight = jnp.sum(lax.all_to_all(share, "context", 0, 0, tiled=True).astype(F32), axis=0)
    dtokens = placed(where, [back[0]] + [swapped(back[i], "dp", 2 * i) for i in (1, 2, 3)])

    v = after(send, *v)
    dqueries, dk_even, dk_own, dk_odd = attention_scores(where, queries, k, v, output_gradient, bias, lse)
    dkeys = collected(dk_even, dk_own, dk_odd)
    return (dqueries, dkeys, dtokens, dweight)


def solution(mesh):
    both = P(("dp", "context"), None)
    in_specs = (both, both, both, both, both, P("dp", None), P("dp", None))
    out_specs = (both, both, both, both)
    return jax.shard_map(shards, mesh=mesh, in_specs=in_specs, out_specs=out_specs, check_vma=False)
```

```python
import math

import jax
import jax.numpy as jnp
from jax import lax
from jax.experimental import pallas as pl
from jax.experimental.pallas import tpu as pltpu
from jax.sharding import PartitionSpec as P

HEAD = 128
LEFT = 128
RIGHT = 64
GROUP = 8
NEG = -1e30
SCALE = 1.0 / math.sqrt(HEAD)
LOG2E = 1.0 / math.log(2.0)
X_CHIPS = 4
Y_CHIPS = 4

BF = jnp.bfloat16
F32 = jnp.float32


def lasting(us):
    return pl.CostEstimate(flops=int(us * 1.1e9), bytes_accessed=1 << 20, transcendentals=0)


def dot(a, b, ca, cb):
    return lax.dot_general(a, b, (((ca,), (cb,)), ((), ())), preferred_element_type=F32)


def visible_bias(first, rows, lengths, offsets):
    slots = lengths.shape[0]
    order = jnp.arange(slots, dtype=jnp.int32)
    ends = jnp.sum(jnp.where(order[None, :] <= order[:, None], lengths[None, :], 0), axis=1)
    starts = ends - lengths
    prefix = jnp.minimum(offsets, lengths)
    position = first + jnp.arange(rows, dtype=jnp.int32)
    ended = ends[:, None] <= position[None, :]
    begun = starts[:, None] <= position[None, :]
    low = jnp.sum(jnp.where(ended, lengths[:, None], 0), axis=0)
    reach = low + jnp.sum(jnp.where(begun & ~ended, prefix[:, None], 0), axis=0)
    high = jnp.maximum(position + 1, reach)
    key = first - LEFT + jnp.arange(LEFT + rows + RIGHT, dtype=jnp.int32)
    seen = (key[:, None] >= low[None, :]) & (key[:, None] < high[None, :])
    return jnp.where(seen, 0.0, NEG).astype(F32)


def stacked(ref):
    return jnp.concatenate([ref[:, h * HEAD : (h + 1) * HEAD] for h in range(GROUP)], axis=0)


def window(odd, even_pair, own, odd_pair):
    left = jnp.where(odd, even_pair[...], odd_pair[...])
    right = jnp.where(odd, odd_pair[...], even_pair[...])
    return jnp.concatenate([left, own[...], right[:RIGHT]], axis=0)


def scatter_window(odd, total, even_pair, own, odd_pair):
    rows = own.shape[0]
    left = total[:LEFT].astype(BF)
    right = total[LEFT + rows :].astype(BF)
    right = jnp.concatenate([right, jnp.zeros((LEFT - RIGHT, right.shape[1]), BF)], axis=0)
    even_pair[...] = jnp.where(odd, left, right)
    own[...] = total[LEFT : LEFT + rows]
    odd_pair[...] = jnp.where(odd, right, left)


def probs_kernel(where_ref, q_ref, ka_ref, ko_ref, kb_ref, g_ref, bias_ref, dva_ref, dvo_ref, dvb_ref, lse_ref):
    odd = where_ref[2] % 2 == 1
    k = window(odd, ka_ref, ko_ref, kb_ref)
    bias = jnp.concatenate([bias_ref[...]] * GROUP, axis=1)
    scores = dot(k, stacked(q_ref), 1, 1) * (SCALE * LOG2E) + bias
    top = jnp.max(scores, axis=0, keepdims=True)
    weights = jnp.exp2(scores - top)
    norm = jnp.sum(weights, axis=0, keepdims=True)
    probs = (weights * (1.0 / norm)).astype(BF)
    lse_ref[0] = top + jnp.log(norm) * LOG2E - math.log2(SCALE)
    scatter_window(odd, dot(probs, stacked(g_ref), 1, 0), dva_ref, dvo_ref, dvb_ref)


def scores_kernel(where_ref, q_ref, ka_ref, ko_ref, kb_ref, va_ref, vo_ref, vb_ref, g_ref, bias_ref, lse_ref, dq_ref, dka_ref, dko_ref, dkb_ref):
    rows = ko_ref.shape[0]
    odd = where_ref[2] % 2 == 1
    k = window(odd, ka_ref, ko_ref, kb_ref)
    v = window(odd, va_ref, vo_ref, vb_ref)
    bias = jnp.concatenate([bias_ref[...]] * GROUP, axis=1)
    q = stacked(q_ref)
    scaled = jnp.exp2(dot(k, q, 1, 1) * (SCALE * LOG2E) + bias - lse_ref[0])
    dprobs = dot(v, stacked(g_ref), 1, 1)
    delta = jnp.sum(scaled * dprobs, axis=0, keepdims=True) * (1.0 / SCALE)
    dscores = (scaled * (dprobs - delta)).astype(BF)
    dq = dot(dscores, k, 0, 0).astype(BF)
    for h in range(GROUP):
        dq_ref[:, h * HEAD : (h + 1) * HEAD] = dq[h * rows : (h + 1) * rows]
    scatter_window(odd, dot(dscores, q, 1, 0), dka_ref, dko_ref, dkb_ref)


def head_spec(rows):
    return pl.BlockSpec((rows, HEAD), lambda g, where: (0, g))


def wide_spec(rows):
    return pl.BlockSpec((rows, GROUP * HEAD), lambda g, where: (0, g))


def lse_spec(rows):
    return pl.BlockSpec((1, 1, GROUP * rows), lambda g, where: (g, 0, 0))


def part_shapes(rows, width):
    pair = jax.ShapeDtypeStruct((LEFT, width), BF)
    return [pair, jax.ShapeDtypeStruct((rows, width), F32), pair]


def window_specs(rows):
    return [head_spec(LEFT), head_spec(rows), head_spec(LEFT)]


def attention_probs(where, q, k, g, bias):
    rows, width = k[1].shape
    heads = width // HEAD
    span = bias.shape[0]
    spec = pltpu.PrefetchScalarGridSpec(
        num_scalar_prefetch=1,
        grid=(heads,),
        in_specs=[wide_spec(rows), *window_specs(rows), wide_spec(rows), pl.BlockSpec((span, rows), lambda g, where: (0, 0))],
        out_specs=[*window_specs(rows), lse_spec(rows)],
    )
    return pl.pallas_call(
        probs_kernel,
        grid_spec=spec,
        out_shape=[*part_shapes(rows, width), jax.ShapeDtypeStruct((heads, 1, GROUP * rows), F32)],
        compiler_params=pltpu.CompilerParams(dimension_semantics=("arbitrary",), vmem_limit_bytes=63 << 20),
        cost_estimate=lasting(6),
        name="probs",
    )(where, q, *k, g, bias)


def attention_scores(where, q, k, v, g, bias, lse):
    rows, width = k[1].shape
    heads = width // HEAD
    span = bias.shape[0]
    spec = pltpu.PrefetchScalarGridSpec(
        num_scalar_prefetch=1,
        grid=(heads,),
        in_specs=[
            wide_spec(rows),
            *window_specs(rows),
            *window_specs(rows),
            wide_spec(rows),
            pl.BlockSpec((span, rows), lambda g, where: (0, 0)),
            lse_spec(rows),
        ],
        out_specs=[wide_spec(rows), *window_specs(rows)],
    )
    return pl.pallas_call(
        scores_kernel,
        grid_spec=spec,
        out_shape=[jax.ShapeDtypeStruct(q.shape, BF), *part_shapes(rows, width)],
        compiler_params=pltpu.CompilerParams(dimension_semantics=("arbitrary",), vmem_limit_bytes=63 << 20),
        cost_estimate=lasting(25),
        name="scores",
    )(where, q, *k, *v, g, bias, lse)


def swapped(x, axis, bits):
    count = lax.axis_size(axis)
    return lax.ppermute(x, axis, [(i, i ^ bits) for i in range(count)])


def pair_swapped(even_pair, odd_pair):
    count = lax.axis_size("context")
    others = [(i, i + 1) for i in range(1, count - 1, 2)]
    others = others + [(b, a) for a, b in others]
    return swapped(even_pair, "context", 1), lax.ppermute(odd_pair, "context", others)


def neighbours(x):
    even_pair, odd_pair = pair_swapped(x, x)
    return (even_pair, x, odd_pair)


def collected(even_pair, own, odd_pair):
    even_pair, odd_pair = pair_swapped(even_pair, odd_pair)
    return (own + even_pair.astype(F32) + odd_pair.astype(F32)).astype(BF)


def split_kernel(where_ref, t1_ref, t2_ref, t3_ref, s1_ref, s2_ref, s3_ref):
    s1_ref[...] = t1_ref[...]
    s2_ref[...] = t2_ref[...]
    s3_ref[...] = t3_ref[...]


def column_spec(rows, width, i):
    return pl.BlockSpec((rows, width), lambda step, where: (0, where[0] ^ i))


def column_blocks(where, tokens):
    rows, width = tokens.shape
    width = width // X_CHIPS
    spec = pltpu.PrefetchScalarGridSpec(
        num_scalar_prefetch=1,
        grid=(1,),
        in_specs=[column_spec(rows, width, i) for i in (1, 2, 3)],
        out_specs=[pl.BlockSpec((rows, width), lambda step, where: (0, 0))] * 3,
    )
    return pl.pallas_call(
        split_kernel,
        grid_spec=spec,
        out_shape=[jax.ShapeDtypeStruct((rows, width), BF)] * 3,
        cost_estimate=lasting(1.5),
        name="split",
    )(where, tokens, tokens, tokens)


def rotated(where_ref, refs):
    high = where_ref[2] // (2 * Y_CHIPS)
    size = refs[0].shape[1] // Y_CHIPS
    at = [pl.multiple_of((high ^ i) * size, size) for i in range(Y_CHIPS)]
    return jnp.concatenate([jnp.concatenate([ref[:, pl.ds(p, size)] for p in at], axis=1) for ref in refs], axis=0)


def project_kernel(where_ref, t0_ref, t1_ref, t2_ref, t3_ref, mine_ref, theirs_ref, part_ref, acc_ref):
    step = pl.program_id(0)
    tokens = rotated(where_ref, (t0_ref, t1_ref, t2_ref, t3_ref))

    @pl.when(step == 0)
    def _():
        acc_ref[...] = dot(tokens, mine_ref[...], 1, 0)

    @pl.when(step == 1)
    def _():
        part = (acc_ref[...] + dot(tokens, theirs_ref[...], 1, 0)).astype(BF)
        rows = part_ref.shape[1]
        for i in range(X_CHIPS):
            part_ref[where_ref[0] ^ i] = part[i * rows : (i + 1) * rows]


def half_specs(rows, depth):
    own = pl.BlockSpec((rows, depth), lambda step, where: (0, where[0] * 2 + (where[1] ^ step)))
    other = pl.BlockSpec((rows, depth), lambda step, where: (0, where[1] ^ step))
    return [own] + [other] * 3


def projected(where, tokens, columns, mine, theirs):
    rows = tokens.shape[0]
    depth, width = mine.shape
    whole = pl.BlockSpec((depth, width), lambda step, where: (0, 0))
    spec = pltpu.PrefetchScalarGridSpec(
        num_scalar_prefetch=1,
        grid=(2,),
        in_specs=half_specs(rows, depth) + [whole, whole],
        out_specs=pl.BlockSpec((X_CHIPS, rows, width), lambda step, where: (0, 0, 0)),
        scratch_shapes=[pltpu.VMEM((X_CHIPS * rows, width), F32)],
    )
    return pl.pallas_call(
        project_kernel,
        grid_spec=spec,
        out_shape=jax.ShapeDtypeStruct((X_CHIPS, rows, width), BF),
        compiler_params=pltpu.CompilerParams(dimension_semantics=("arbitrary",), vmem_limit_bytes=63 << 20),
        cost_estimate=lasting(4),
        name="project",
    )(where, tokens, *columns, mine, theirs)


def weight_kernel(where_ref, t0_ref, t1_ref, t2_ref, t3_ref, d0_ref, d1_ref, d2_ref, d3_ref, mine_ref, theirs_ref, send_ref, keep_ref, *back_refs):
    step = pl.program_id(0)
    tokens = jnp.concatenate([t0_ref[...], t1_ref[...], t2_ref[...], t3_ref[...]], axis=0)
    dvalues = jnp.concatenate([d0_ref[...], d1_ref[...], d2_ref[...], d3_ref[...]], axis=0)
    part = dot(tokens, dvalues, 0, 0)
    rows = d0_ref.shape[0]
    high = where_ref[2] // (2 * Y_CHIPS)

    def store(back):
        size = back.shape[1] // Y_CHIPS
        for i, ref in enumerate(back_refs):
            for j in range(Y_CHIPS):
                at = pl.multiple_of((high ^ j) * size, size)
                ref[:, pl.ds(at, size)] = back[i * rows : (i + 1) * rows, j * size : (j + 1) * size].astype(BF)

    @pl.when(step == 0)
    def _():
        send_ref[...] = part.astype(BF)
        store(dot(dvalues, theirs_ref[...], 1, 1))

    @pl.when(step == 1)
    def _():
        keep_ref[...] = part.astype(BF)
        store(dot(dvalues, mine_ref[...], 1, 1))


def weight_partials(where, tokens, columns, dvalues, mine, theirs):
    rows = tokens.shape[0]
    depth, width = mine.shape
    whole = pl.BlockSpec((depth, width), lambda step, where: (0, 0))
    part = pl.BlockSpec((rows, width), lambda step, where: (0, 0))
    own = pl.BlockSpec((rows, depth), lambda step, where: (0, where[0] * 2 + (1 - (where[1] ^ step))))
    other = pl.BlockSpec((rows, depth), lambda step, where: (0, 1 - (where[1] ^ step)))
    spec = pltpu.PrefetchScalarGridSpec(
        num_scalar_prefetch=1,
        grid=(2,),
        in_specs=[own] + [other] * 3 + [part] * 4 + [whole, whole],
        out_specs=[whole, whole] + [other] * 4,
    )
    return pl.pallas_call(
        weight_kernel,
        grid_spec=spec,
        out_shape=[jax.ShapeDtypeStruct((depth, width), BF)] * 2
        + [jax.ShapeDtypeStruct((rows, 2 * depth), BF)] * 4,
        compiler_params=pltpu.CompilerParams(dimension_semantics=("arbitrary",), vmem_limit_bytes=63 << 20),
        cost_estimate=lasting(5),
        name="weights",
    )(where, tokens, *columns, *dvalues, mine, theirs)


def place_kernel(where_ref, t0_ref, t1_ref, t2_ref, t3_ref, out_ref):
    width = t0_ref.shape[1]
    for i, ref in enumerate((t0_ref, t1_ref, t2_ref, t3_ref)):
        at = pl.multiple_of((where_ref[0] ^ i) * width, width)
        out_ref[:, pl.ds(at, width)] = ref[...]


def placed(where, pieces):
    rows, width = pieces[0].shape
    return pl.pallas_call(
        place_kernel,
        in_specs=[pl.BlockSpec(memory_space=pltpu.SMEM)] + [pl.BlockSpec(memory_space=pltpu.VMEM)] * 4,
        out_specs=pl.BlockSpec(memory_space=pltpu.VMEM),
        out_shape=jax.ShapeDtypeStruct((rows, X_CHIPS * width), BF),
        cost_estimate=lasting(2.4),
        name="place",
    )(where, *pieces)


def after(earlier, *later):
    return lax.optimization_barrier((later, earlier))[0]


def shards(queries, keys, tokens, value_matrix, output_gradient, segment_lengths, segment_offsets):
    rows = queries.shape[0]
    place = lax.axis_index("context")
    dp = lax.axis_index("dp")
    contexts = lax.axis_size("context")
    where = jnp.stack([dp // 2, dp % 2, place]).astype(jnp.int32)
    bias = visible_bias(place * rows, rows, segment_lengths[0], segment_offsets[0])

    rings = contexts // Y_CHIPS
    along_z = [[y * rings + z for z in range(rings)] for y in range(Y_CHIPS)]
    copies = jnp.broadcast_to(value_matrix[None], (rings,) + value_matrix.shape)
    ring = lax.all_to_all(copies, "context", 0, 0, axis_index_groups=along_z, tiled=True)
    (moving_tokens,) = after(copies, tokens)
    sent = column_blocks(where, moving_tokens)
    columns = [swapped(sent[i - 1], "dp", 2 * i) for i in (1, 2, 3)]
    ring = ring.reshape(rings * value_matrix.shape[0], value_matrix.shape[1])
    mine = jnp.concatenate([ring] + [swapped(ring, "context", rings * i) for i in (1, 2, 3)], axis=0)
    theirs = swapped(mine, "dp", 1)
    (moving_keys,) = after(sent, keys)
    k_even, unused, k_odd = neighbours(moving_keys)
    k = (k_even, keys, k_odd)
    (bias,) = after(mine, bias)

    dv_even, dv_own, dv_odd, lse = attention_probs(where, queries, k, output_gradient, bias)
    dv_even, dv_odd = after((columns, mine), dv_even, dv_odd)
    dvalues = collected(dv_even, dv_own, dv_odd)
    all_dvalues = [dvalues] + [swapped(dvalues, "dp", 2 * i) for i in (1, 2, 3)]

    groups = [[2 * x + core for x in range(X_CHIPS)] for core in range(2)]
    started = projected(where, tokens, columns, mine, theirs)
    parts = lax.all_to_all(started, "dp", 0, 0, axis_index_groups=groups, tiled=True)
    values = jnp.sum(parts.astype(F32), axis=0).astype(BF)
    v = neighbours(values)

    all_dvalues = after(started, *all_dvalues)
    send, keep, *back = weight_partials(where, tokens, columns, all_dvalues, mine, theirs)
    share = (keep.astype(F32) + swapped(send, "dp", 1).astype(F32)).astype(BF)
    share = share.reshape(contexts, -1, share.shape[1])
    share = lax.all_to_all(share, "context", 0, 0, tiled=True)
    dweight = jnp.sum(share.astype(F32), axis=0)
    back = [back[0]] + [swapped(back[i], "dp", 2 * i) for i in (1, 2, 3)]
    dtokens = placed(where, back)

    v = after(send, *v)
    dqueries, dk_even, dk_own, dk_odd = attention_scores(where, queries, k, v, output_gradient, bias, lse)
    dkeys = collected(dk_even, dk_own, dk_odd)
    return (dqueries, dkeys, dtokens, dweight)


def solution(mesh):
    both = P(("dp", "context"), None)
    in_specs = (both, both, both, both, both, P("dp", None), P("dp", None))
    out_specs = (both, both, both, both)
    return jax.shard_map(shards, mesh=mesh, in_specs=in_specs, out_specs=out_specs, check_vma=False)
```

```python
import math

import jax
import jax.numpy as jnp
from jax import lax
from jax.experimental import pallas as pl
from jax.experimental.pallas import tpu as pltpu
from jax.sharding import PartitionSpec as P

HEAD = 128
LEFT = 128
RIGHT = 64
GROUP = 8
NEG = -1e30
SCALE = 1.0 / math.sqrt(HEAD)
LOG2E = 1.0 / math.log(2.0)
X_CHIPS = 4
Y_CHIPS = 4

BF = jnp.bfloat16
F32 = jnp.float32


def lasting(us):
    return pl.CostEstimate(flops=int(us * 1.1e9), bytes_accessed=1 << 20, transcendentals=0)


def dot(a, b, ca, cb):
    return lax.dot_general(a, b, (((ca,), (cb,)), ((), ())), preferred_element_type=F32)


def visible_bias(first, rows, lengths, offsets):
    slots = lengths.shape[0]
    order = jnp.arange(slots, dtype=jnp.int32)
    ends = jnp.sum(jnp.where(order[None, :] <= order[:, None], lengths[None, :], 0), axis=1)
    starts = ends - lengths
    prefix = jnp.minimum(offsets, lengths)
    position = first + jnp.arange(rows, dtype=jnp.int32)
    ended = ends[:, None] <= position[None, :]
    begun = starts[:, None] <= position[None, :]
    low = jnp.sum(jnp.where(ended, lengths[:, None], 0), axis=0)
    reach = low + jnp.sum(jnp.where(begun & ~ended, prefix[:, None], 0), axis=0)
    high = jnp.maximum(position + 1, reach)
    key = first - LEFT + jnp.arange(LEFT + rows + RIGHT, dtype=jnp.int32)
    seen = (key[:, None] >= low[None, :]) & (key[:, None] < high[None, :])
    return jnp.where(seen, 0.0, NEG).astype(F32)


def stacked(ref):
    return jnp.concatenate([ref[:, h * HEAD : (h + 1) * HEAD] for h in range(GROUP)], axis=0)


def window(odd, even_pair, own, odd_pair):
    left = jnp.where(odd, even_pair[...], odd_pair[...])
    right = jnp.where(odd, odd_pair[...], even_pair[...])
    return jnp.concatenate([left, own[...], right[:RIGHT]], axis=0)


def scatter_window(odd, total, even_pair, own, odd_pair):
    rows = own.shape[0]
    left = total[:LEFT].astype(BF)
    right = total[LEFT + rows :].astype(BF)
    right = jnp.concatenate([right, jnp.zeros((LEFT - RIGHT, right.shape[1]), BF)], axis=0)
    even_pair[...] = jnp.where(odd, left, right)
    own[...] = total[LEFT : LEFT + rows]
    odd_pair[...] = jnp.where(odd, right, left)


def probs_kernel(where_ref, q_ref, ka_ref, ko_ref, kb_ref, g_ref, bias_ref, dva_ref, dvo_ref, dvb_ref, lse_ref):
    odd = where_ref[2] % 2 == 1
    k = window(odd, ka_ref, ko_ref, kb_ref)
    bias = jnp.concatenate([bias_ref[...]] * GROUP, axis=1)
    scores = dot(k, stacked(q_ref), 1, 1) * (SCALE * LOG2E) + bias
    top = jnp.max(scores, axis=0, keepdims=True)
    weights = jnp.exp2(scores - top)
    norm = jnp.sum(weights, axis=0, keepdims=True)
    probs = (weights * (1.0 / norm)).astype(BF)
    lse_ref[0] = top + jnp.log(norm) * LOG2E - math.log2(SCALE)
    scatter_window(odd, dot(probs, stacked(g_ref), 1, 0), dva_ref, dvo_ref, dvb_ref)


def scores_kernel(where_ref, q_ref, ka_ref, ko_ref, kb_ref, va_ref, vo_ref, vb_ref, g_ref, bias_ref, lse_ref, dq_ref, dka_ref, dko_ref, dkb_ref):
    rows = ko_ref.shape[0]
    odd = where_ref[2] % 2 == 1
    k = window(odd, ka_ref, ko_ref, kb_ref)
    v = window(odd, va_ref, vo_ref, vb_ref)
    bias = jnp.concatenate([bias_ref[...]] * GROUP, axis=1)
    q = stacked(q_ref)
    scaled = jnp.exp2(dot(k, q, 1, 1) * (SCALE * LOG2E) + bias - lse_ref[0])
    dprobs = dot(v, stacked(g_ref), 1, 1)
    delta = jnp.sum(scaled * dprobs, axis=0, keepdims=True) * (1.0 / SCALE)
    dscores = (scaled * (dprobs - delta)).astype(BF)
    dq = dot(dscores, k, 0, 0).astype(BF)
    for h in range(GROUP):
        dq_ref[:, h * HEAD : (h + 1) * HEAD] = dq[h * rows : (h + 1) * rows]
    scatter_window(odd, dot(dscores, q, 1, 0), dka_ref, dko_ref, dkb_ref)


def head_spec(rows):
    return pl.BlockSpec((rows, HEAD), lambda g, where: (0, g))


def wide_spec(rows):
    return pl.BlockSpec((rows, GROUP * HEAD), lambda g, where: (0, g))


def lse_spec(rows):
    return pl.BlockSpec((1, 1, GROUP * rows), lambda g, where: (g, 0, 0))


def part_shapes(rows, width):
    pair = jax.ShapeDtypeStruct((LEFT, width), BF)
    return [pair, jax.ShapeDtypeStruct((rows, width), F32), pair]


def window_specs(rows):
    return [head_spec(LEFT), head_spec(rows), head_spec(LEFT)]


def attention_probs(where, q, k, g, bias):
    rows, width = k[1].shape
    heads = width // HEAD
    span = bias.shape[0]
    spec = pltpu.PrefetchScalarGridSpec(
        num_scalar_prefetch=1,
        grid=(heads,),
        in_specs=[wide_spec(rows), *window_specs(rows), wide_spec(rows), pl.BlockSpec((span, rows), lambda g, where: (0, 0))],
        out_specs=[*window_specs(rows), lse_spec(rows)],
    )
    return pl.pallas_call(
        probs_kernel,
        grid_spec=spec,
        out_shape=[*part_shapes(rows, width), jax.ShapeDtypeStruct((heads, 1, GROUP * rows), F32)],
        compiler_params=pltpu.CompilerParams(dimension_semantics=("arbitrary",), vmem_limit_bytes=63 << 20),
        cost_estimate=lasting(6),
        name="probs",
    )(where, q, *k, g, bias)


def attention_scores(where, q, k, v, g, bias, lse):
    rows, width = k[1].shape
    heads = width // HEAD
    span = bias.shape[0]
    spec = pltpu.PrefetchScalarGridSpec(
        num_scalar_prefetch=1,
        grid=(heads,),
        in_specs=[
            wide_spec(rows),
            *window_specs(rows),
            *window_specs(rows),
            wide_spec(rows),
            pl.BlockSpec((span, rows), lambda g, where: (0, 0)),
            lse_spec(rows),
        ],
        out_specs=[wide_spec(rows), *window_specs(rows)],
    )
    return pl.pallas_call(
        scores_kernel,
        grid_spec=spec,
        out_shape=[jax.ShapeDtypeStruct(q.shape, BF), *part_shapes(rows, width)],
        compiler_params=pltpu.CompilerParams(dimension_semantics=("arbitrary",), vmem_limit_bytes=63 << 20),
        cost_estimate=lasting(25),
        name="scores",
    )(where, q, *k, *v, g, bias, lse)


def swapped(x, axis, bits):
    count = lax.axis_size(axis)
    return lax.ppermute(x, axis, [(i, i ^ bits) for i in range(count)])


def pair_swapped(even_pair, odd_pair):
    count = lax.axis_size("context")
    others = [(i, i + 1) for i in range(1, count - 1, 2)]
    others = others + [(b, a) for a, b in others]
    return swapped(even_pair, "context", 1), lax.ppermute(odd_pair, "context", others)


def neighbours(x):
    even_pair, odd_pair = pair_swapped(x, x)
    return (even_pair, x, odd_pair)


def collected(even_pair, own, odd_pair):
    even_pair, odd_pair = pair_swapped(even_pair, odd_pair)
    return (own + even_pair.astype(F32) + odd_pair.astype(F32)).astype(BF)


def split_kernel(where_ref, t1_ref, t2_ref, t3_ref, s1_ref, s2_ref, s3_ref):
    s1_ref[...] = t1_ref[...]
    s2_ref[...] = t2_ref[...]
    s3_ref[...] = t3_ref[...]


def column_spec(rows, width, i):
    return pl.BlockSpec((rows, width), lambda step, where: (0, where[0] ^ i))


def column_blocks(where, tokens):
    rows, width = tokens.shape
    width = width // X_CHIPS
    spec = pltpu.PrefetchScalarGridSpec(
        num_scalar_prefetch=1,
        grid=(1,),
        in_specs=[column_spec(rows, width, i) for i in (1, 2, 3)],
        out_specs=[pl.BlockSpec((rows, width), lambda step, where: (0, 0))] * 3,
    )
    return pl.pallas_call(
        split_kernel,
        grid_spec=spec,
        out_shape=[jax.ShapeDtypeStruct((rows, width), BF)] * 3,
        cost_estimate=lasting(1.5),
        name="split",
    )(where, tokens, tokens, tokens)


def rotated(where_ref, refs):
    high = where_ref[2] // (2 * Y_CHIPS)
    size = refs[0].shape[1] // Y_CHIPS
    at = [pl.multiple_of((high ^ i) * size, size) for i in range(Y_CHIPS)]
    return jnp.concatenate([jnp.concatenate([ref[:, pl.ds(p, size)] for p in at], axis=1) for ref in refs], axis=0)


def project_kernel(where_ref, t0_ref, t1_ref, t2_ref, t3_ref, mine_ref, theirs_ref, part_ref, acc_ref):
    step = pl.program_id(0)
    tokens = rotated(where_ref, (t0_ref, t1_ref, t2_ref, t3_ref))

    @pl.when(step == 0)
    def _():
        acc_ref[...] = dot(tokens, mine_ref[...], 1, 0)

    @pl.when(step == 1)
    def _():
        part = (acc_ref[...] + dot(tokens, theirs_ref[...], 1, 0)).astype(BF)
        rows = part_ref.shape[1]
        for i in range(X_CHIPS):
            part_ref[where_ref[0] ^ i] = part[i * rows : (i + 1) * rows]


def half_specs(rows, depth):
    own = pl.BlockSpec((rows, depth), lambda step, where: (0, where[0] * 2 + (where[1] ^ step)))
    other = pl.BlockSpec((rows, depth), lambda step, where: (0, where[1] ^ step))
    return [own] + [other] * 3


def projected(where, tokens, columns, mine, theirs):
    rows = tokens.shape[0]
    depth, width = mine.shape
    whole = pl.BlockSpec((depth, width), lambda step, where: (0, 0))
    spec = pltpu.PrefetchScalarGridSpec(
        num_scalar_prefetch=1,
        grid=(2,),
        in_specs=half_specs(rows, depth) + [whole, whole],
        out_specs=pl.BlockSpec((X_CHIPS, rows, width), lambda step, where: (0, 0, 0)),
        scratch_shapes=[pltpu.VMEM((X_CHIPS * rows, width), F32)],
    )
    return pl.pallas_call(
        project_kernel,
        grid_spec=spec,
        out_shape=jax.ShapeDtypeStruct((X_CHIPS, rows, width), BF),
        compiler_params=pltpu.CompilerParams(dimension_semantics=("arbitrary",), vmem_limit_bytes=63 << 20),
        cost_estimate=lasting(4),
        name="project",
    )(where, tokens, *columns, mine, theirs)


def weight_kernel(where_ref, t0_ref, t1_ref, t2_ref, t3_ref, d0_ref, d1_ref, d2_ref, d3_ref, mine_ref, theirs_ref, send_ref, keep_ref, *back_refs):
    step = pl.program_id(0)
    tokens = jnp.concatenate([t0_ref[...], t1_ref[...], t2_ref[...], t3_ref[...]], axis=0)
    dvalues = jnp.concatenate([d0_ref[...], d1_ref[...], d2_ref[...], d3_ref[...]], axis=0)
    part = dot(tokens, dvalues, 0, 0)
    rows = d0_ref.shape[0]
    high = where_ref[2] // (2 * Y_CHIPS)

    def store(back):
        size = back.shape[1] // Y_CHIPS
        for i, ref in enumerate(back_refs):
            for j in range(Y_CHIPS):
                at = pl.multiple_of((high ^ j) * size, size)
                ref[:, pl.ds(at, size)] = back[i * rows : (i + 1) * rows, j * size : (j + 1) * size].astype(BF)

    @pl.when(step == 0)
    def _():
        send_ref[...] = part.astype(BF)
        store(dot(dvalues, theirs_ref[...], 1, 1))

    @pl.when(step == 1)
    def _():
        keep_ref[...] = part.astype(BF)
        store(dot(dvalues, mine_ref[...], 1, 1))


def weight_partials(where, tokens, columns, dvalues, mine, theirs):
    rows = tokens.shape[0]
    depth, width = mine.shape
    whole = pl.BlockSpec((depth, width), lambda step, where: (0, 0))
    part = pl.BlockSpec((rows, width), lambda step, where: (0, 0))
    own = pl.BlockSpec((rows, depth), lambda step, where: (0, where[0] * 2 + (1 - (where[1] ^ step))))
    other = pl.BlockSpec((rows, depth), lambda step, where: (0, 1 - (where[1] ^ step)))
    spec = pltpu.PrefetchScalarGridSpec(
        num_scalar_prefetch=1,
        grid=(2,),
        in_specs=[own] + [other] * 3 + [part] * 4 + [whole, whole],
        out_specs=[whole, whole] + [other] * 4,
    )
    return pl.pallas_call(
        weight_kernel,
        grid_spec=spec,
        out_shape=[jax.ShapeDtypeStruct((depth, width), BF)] * 2
        + [jax.ShapeDtypeStruct((rows, 2 * depth), BF)] * 4,
        compiler_params=pltpu.CompilerParams(dimension_semantics=("arbitrary",), vmem_limit_bytes=63 << 20),
        cost_estimate=lasting(5),
        name="weights",
    )(where, tokens, *columns, *dvalues, mine, theirs)


def place_kernel(where_ref, t0_ref, t1_ref, t2_ref, t3_ref, out_ref):
    width = t0_ref.shape[1]
    for i, ref in enumerate((t0_ref, t1_ref, t2_ref, t3_ref)):
        at = pl.multiple_of((where_ref[0] ^ i) * width, width)
        out_ref[:, pl.ds(at, width)] = ref[...]


def placed(where, pieces):
    rows, width = pieces[0].shape
    return pl.pallas_call(
        place_kernel,
        in_specs=[pl.BlockSpec(memory_space=pltpu.SMEM)] + [pl.BlockSpec(memory_space=pltpu.VMEM)] * 4,
        out_specs=pl.BlockSpec(memory_space=pltpu.VMEM),
        out_shape=jax.ShapeDtypeStruct((rows, X_CHIPS * width), BF),
        cost_estimate=lasting(2.4),
        name="place",
    )(where, *pieces)


def after(earlier, *later):
    return lax.optimization_barrier((later, earlier))[0]


def shards(queries, keys, tokens, value_matrix, output_gradient, segment_lengths, segment_offsets):
    rows = queries.shape[0]
    place = lax.axis_index("context")
    dp = lax.axis_index("dp")
    contexts = lax.axis_size("context")
    where = jnp.stack([dp // 2, dp % 2, place]).astype(jnp.int32)
    bias = visible_bias(place * rows, rows, segment_lengths[0], segment_offsets[0])

    rings = contexts // Y_CHIPS
    along_z = [[y * rings + z for z in range(rings)] for y in range(Y_CHIPS)]
    copies = jnp.broadcast_to(value_matrix[None], (rings,) + value_matrix.shape)
    ring = lax.all_to_all(copies, "context", 0, 0, axis_index_groups=along_z, tiled=True)
    (moving_tokens,) = after(copies, tokens)
    sent = column_blocks(where, moving_tokens)
    columns = [swapped(sent[i - 1], "dp", 2 * i) for i in (1, 2, 3)]
    ring = ring.reshape(rings * value_matrix.shape[0], value_matrix.shape[1])
    mine = jnp.concatenate([ring] + [swapped(ring, "context", rings * i) for i in (1, 2, 3)], axis=0)
    theirs = swapped(mine, "dp", 1)
    (moving_keys,) = after(sent, keys)
    k_even, unused, k_odd = neighbours(moving_keys)
    k = (k_even, keys, k_odd)
    (bias,) = after((columns[0], ring), bias)

    dv_even, dv_own, dv_odd, lse = attention_probs(where, queries, k, output_gradient, bias)
    dv_even, dv_odd = after((columns, mine), dv_even, dv_odd)
    dvalues = collected(dv_even, dv_own, dv_odd)
    all_dvalues = [dvalues] + [swapped(dvalues, "dp", 2 * i) for i in (1, 2, 3)]

    groups = [[2 * x + core for x in range(X_CHIPS)] for core in range(2)]
    started = projected(where, tokens, columns, mine, theirs)
    parts = lax.all_to_all(started, "dp", 0, 0, axis_index_groups=groups, tiled=True)
    values = jnp.sum(parts.astype(F32), axis=0).astype(BF)
    v = neighbours(values)

    all_dvalues = after(started, *all_dvalues)
    send, keep, *back = weight_partials(where, tokens, columns, all_dvalues, mine, theirs)
    share = (keep.astype(F32) + swapped(send, "dp", 1).astype(F32)).astype(BF)
    share = share.reshape(contexts, -1, share.shape[1])
    share = lax.all_to_all(share, "context", 0, 0, tiled=True)
    dweight = jnp.sum(share.astype(F32), axis=0)
    back = [back[0]] + [swapped(back[i], "dp", 2 * i) for i in (1, 2, 3)]
    dtokens = placed(where, back)

    v = after(send, *v)
    dqueries, dk_even, dk_own, dk_odd = attention_scores(where, queries, k, v, output_gradient, bias, lse)
    dkeys = collected(dk_even, dk_own, dk_odd)
    return (dqueries, dkeys, dtokens, dweight)


def solution(mesh):
    both = P(("dp", "context"), None)
    in_specs = (both, both, both, both, both, P("dp", None), P("dp", None))
    out_specs = (both, both, both, both)
    return jax.shard_map(shards, mesh=mesh, in_specs=in_specs, out_specs=out_specs, check_vma=False)
```

```python
import math

import jax
import jax.numpy as jnp
from jax import lax
from jax.experimental import pallas as pl
from jax.experimental.pallas import tpu as pltpu
from jax.sharding import PartitionSpec as P

HEAD = 128
LEFT = 128
RIGHT = 64
GROUP = 8
NEG = -1e30
SCALE = 1.0 / math.sqrt(HEAD)
LOG2E = 1.0 / math.log(2.0)
X_CHIPS = 4
Y_CHIPS = 4

BF = jnp.bfloat16
F32 = jnp.float32


def lasting(us):
    return pl.CostEstimate(flops=int(us * 1.1e9), bytes_accessed=1 << 20, transcendentals=0)


def dot(a, b, ca, cb):
    return lax.dot_general(a, b, (((ca,), (cb,)), ((), ())), preferred_element_type=F32)


def visible_bias(first, rows, lengths, offsets):
    slots = lengths.shape[0]
    order = jnp.arange(slots, dtype=jnp.int32)
    ends = jnp.sum(jnp.where(order[None, :] <= order[:, None], lengths[None, :], 0), axis=1)
    starts = ends - lengths
    prefix = jnp.minimum(offsets, lengths)
    position = first + jnp.arange(rows, dtype=jnp.int32)
    ended = ends[:, None] <= position[None, :]
    begun = starts[:, None] <= position[None, :]
    low = jnp.sum(jnp.where(ended, lengths[:, None], 0), axis=0)
    reach = low + jnp.sum(jnp.where(begun & ~ended, prefix[:, None], 0), axis=0)
    high = jnp.maximum(position + 1, reach)
    key = first - LEFT + jnp.arange(LEFT + rows + RIGHT, dtype=jnp.int32)
    seen = (key[:, None] >= low[None, :]) & (key[:, None] < high[None, :])
    return jnp.where(seen, 0.0, NEG).astype(F32)


def stacked(ref):
    return jnp.concatenate([ref[:, h * HEAD : (h + 1) * HEAD] for h in range(GROUP)], axis=0)


def window(odd, even_pair, own, odd_pair):
    left = jnp.where(odd, even_pair[...], odd_pair[...])
    right = jnp.where(odd, odd_pair[...], even_pair[...])
    return jnp.concatenate([left, own[...], right[:RIGHT]], axis=0)


def scatter_window(odd, total, even_pair, own, odd_pair):
    rows = own.shape[0]
    left = total[:LEFT].astype(BF)
    right = total[LEFT + rows :].astype(BF)
    right = jnp.concatenate([right, jnp.zeros((LEFT - RIGHT, right.shape[1]), BF)], axis=0)
    even_pair[...] = jnp.where(odd, left, right)
    own[...] = total[LEFT : LEFT + rows]
    odd_pair[...] = jnp.where(odd, right, left)


def probs_kernel(where_ref, q_ref, ka_ref, ko_ref, kb_ref, g_ref, bias_ref, dva_ref, dvo_ref, dvb_ref, lse_ref):
    odd = where_ref[2] % 2 == 1
    k = window(odd, ka_ref, ko_ref, kb_ref)
    bias = jnp.concatenate([bias_ref[...]] * GROUP, axis=1)
    scores = dot(k, stacked(q_ref), 1, 1) * (SCALE * LOG2E) + bias
    top = jnp.max(scores, axis=0, keepdims=True)
    weights = jnp.exp2(scores - top)
    norm = jnp.sum(weights, axis=0, keepdims=True)
    probs = (weights * (1.0 / norm)).astype(BF)
    lse_ref[0] = top + jnp.log(norm) * LOG2E - math.log2(SCALE)
    scatter_window(odd, dot(probs, stacked(g_ref), 1, 0), dva_ref, dvo_ref, dvb_ref)


def scores_kernel(where_ref, q_ref, ka_ref, ko_ref, kb_ref, va_ref, vo_ref, vb_ref, g_ref, bias_ref, lse_ref, dq_ref, dka_ref, dko_ref, dkb_ref):
    rows = ko_ref.shape[0]
    odd = where_ref[2] % 2 == 1
    k = window(odd, ka_ref, ko_ref, kb_ref)
    v = window(odd, va_ref, vo_ref, vb_ref)
    bias = jnp.concatenate([bias_ref[...]] * GROUP, axis=1)
    q = stacked(q_ref)
    scaled = jnp.exp2(dot(k, q, 1, 1) * (SCALE * LOG2E) + bias - lse_ref[0])
    dprobs = dot(v, stacked(g_ref), 1, 1)
    delta = jnp.sum(scaled * dprobs, axis=0, keepdims=True) * (1.0 / SCALE)
    dscores = (scaled * (dprobs - delta)).astype(BF)
    dq = dot(dscores, k, 0, 0).astype(BF)
    for h in range(GROUP):
        dq_ref[:, h * HEAD : (h + 1) * HEAD] = dq[h * rows : (h + 1) * rows]
    scatter_window(odd, dot(dscores, q, 1, 0), dka_ref, dko_ref, dkb_ref)


def head_spec(rows):
    return pl.BlockSpec((rows, HEAD), lambda g, where: (0, g))


def wide_spec(rows):
    return pl.BlockSpec((rows, GROUP * HEAD), lambda g, where: (0, g))


def lse_spec(rows):
    return pl.BlockSpec((1, 1, GROUP * rows), lambda g, where: (g, 0, 0))


def part_shapes(rows, width):
    pair = jax.ShapeDtypeStruct((LEFT, width), BF)
    return [pair, jax.ShapeDtypeStruct((rows, width), F32), pair]


def window_specs(rows):
    return [head_spec(LEFT), head_spec(rows), head_spec(LEFT)]


def attention_probs(where, q, k, g, bias):
    rows, width = k[1].shape
    heads = width // HEAD
    span = bias.shape[0]
    spec = pltpu.PrefetchScalarGridSpec(
        num_scalar_prefetch=1,
        grid=(heads,),
        in_specs=[wide_spec(rows), *window_specs(rows), wide_spec(rows), pl.BlockSpec((span, rows), lambda g, where: (0, 0))],
        out_specs=[*window_specs(rows), lse_spec(rows)],
    )
    return pl.pallas_call(
        probs_kernel,
        grid_spec=spec,
        out_shape=[*part_shapes(rows, width), jax.ShapeDtypeStruct((heads, 1, GROUP * rows), F32)],
        compiler_params=pltpu.CompilerParams(dimension_semantics=("arbitrary",), vmem_limit_bytes=63 << 20),
        cost_estimate=lasting(6),
        name="probs",
    )(where, q, *k, g, bias)


def attention_scores(where, q, k, v, g, bias, lse):
    rows, width = k[1].shape
    heads = width // HEAD
    span = bias.shape[0]
    spec = pltpu.PrefetchScalarGridSpec(
        num_scalar_prefetch=1,
        grid=(heads,),
        in_specs=[
            wide_spec(rows),
            *window_specs(rows),
            *window_specs(rows),
            wide_spec(rows),
            pl.BlockSpec((span, rows), lambda g, where: (0, 0)),
            lse_spec(rows),
        ],
        out_specs=[wide_spec(rows), *window_specs(rows)],
    )
    return pl.pallas_call(
        scores_kernel,
        grid_spec=spec,
        out_shape=[jax.ShapeDtypeStruct(q.shape, BF), *part_shapes(rows, width)],
        compiler_params=pltpu.CompilerParams(dimension_semantics=("arbitrary",), vmem_limit_bytes=63 << 20),
        cost_estimate=lasting(25),
        name="scores",
    )(where, q, *k, *v, g, bias, lse)


def swapped(x, axis, bits):
    count = lax.axis_size(axis)
    return lax.ppermute(x, axis, [(i, i ^ bits) for i in range(count)])


def pair_swapped(even_pair, odd_pair):
    count = lax.axis_size("context")
    others = [(i, i + 1) for i in range(1, count - 1, 2)]
    others = others + [(b, a) for a, b in others]
    return swapped(even_pair, "context", 1), lax.ppermute(odd_pair, "context", others)


def neighbours(x):
    even_pair, odd_pair = pair_swapped(x, x)
    return (even_pair, x, odd_pair)


def collected(even_pair, own, odd_pair):
    even_pair, odd_pair = pair_swapped(even_pair, odd_pair)
    return (own + even_pair.astype(F32) + odd_pair.astype(F32)).astype(BF)


def split_kernel(where_ref, t1_ref, t2_ref, t3_ref, s1_ref, s2_ref, s3_ref):
    s1_ref[...] = t1_ref[...]
    s2_ref[...] = t2_ref[...]
    s3_ref[...] = t3_ref[...]


def column_spec(rows, width, i):
    return pl.BlockSpec((rows, width), lambda step, where: (0, where[0] ^ i))


def column_blocks(where, tokens):
    rows, width = tokens.shape
    width = width // X_CHIPS
    spec = pltpu.PrefetchScalarGridSpec(
        num_scalar_prefetch=1,
        grid=(1,),
        in_specs=[column_spec(rows, width, i) for i in (1, 2, 3)],
        out_specs=[pl.BlockSpec((rows, width), lambda step, where: (0, 0))] * 3,
    )
    return pl.pallas_call(
        split_kernel,
        grid_spec=spec,
        out_shape=[jax.ShapeDtypeStruct((rows, width), BF)] * 3,
        cost_estimate=lasting(1.5),
        name="split",
    )(where, tokens, tokens, tokens)


def rotated(where_ref, refs):
    high = where_ref[2] // (2 * Y_CHIPS)
    size = refs[0].shape[1] // Y_CHIPS
    at = [pl.multiple_of((high ^ i) * size, size) for i in range(Y_CHIPS)]
    return jnp.concatenate([jnp.concatenate([ref[:, pl.ds(p, size)] for p in at], axis=1) for ref in refs], axis=0)


def project_kernel(where_ref, t0_ref, t1_ref, t2_ref, t3_ref, mine_ref, theirs_ref, part_ref, acc_ref):
    step = pl.program_id(0)
    tokens = rotated(where_ref, (t0_ref, t1_ref, t2_ref, t3_ref))

    @pl.when(step == 0)
    def _():
        acc_ref[...] = dot(tokens, mine_ref[...], 1, 0)

    @pl.when(step == 1)
    def _():
        part = (acc_ref[...] + dot(tokens, theirs_ref[...], 1, 0)).astype(BF)
        rows = part_ref.shape[1]
        for i in range(X_CHIPS):
            part_ref[where_ref[0] ^ i] = part[i * rows : (i + 1) * rows]


def half_specs(rows, depth):
    own = pl.BlockSpec((rows, depth), lambda step, where: (0, where[0] * 2 + (where[1] ^ step)))
    other = pl.BlockSpec((rows, depth), lambda step, where: (0, where[1] ^ step))
    return [own] + [other] * 3


def projected(where, tokens, columns, mine, theirs):
    rows = tokens.shape[0]
    depth, width = mine.shape
    whole = pl.BlockSpec((depth, width), lambda step, where: (0, 0))
    spec = pltpu.PrefetchScalarGridSpec(
        num_scalar_prefetch=1,
        grid=(2,),
        in_specs=half_specs(rows, depth) + [whole, whole],
        out_specs=pl.BlockSpec((X_CHIPS, rows, width), lambda step, where: (0, 0, 0)),
        scratch_shapes=[pltpu.VMEM((X_CHIPS * rows, width), F32)],
    )
    return pl.pallas_call(
        project_kernel,
        grid_spec=spec,
        out_shape=jax.ShapeDtypeStruct((X_CHIPS, rows, width), BF),
        compiler_params=pltpu.CompilerParams(dimension_semantics=("arbitrary",), vmem_limit_bytes=63 << 20),
        cost_estimate=lasting(4),
        name="project",
    )(where, tokens, *columns, mine, theirs)


def weight_kernel(where_ref, t0_ref, t1_ref, t2_ref, t3_ref, d0_ref, d1_ref, d2_ref, d3_ref, mine_ref, theirs_ref, send_ref, keep_ref, *back_refs):
    step = pl.program_id(0)
    tokens = jnp.concatenate([t0_ref[...], t1_ref[...], t2_ref[...], t3_ref[...]], axis=0)
    dvalues = jnp.concatenate([d0_ref[...], d1_ref[...], d2_ref[...], d3_ref[...]], axis=0)
    part = dot(tokens, dvalues, 0, 0)
    rows = d0_ref.shape[0]
    high = where_ref[2] // (2 * Y_CHIPS)

    def store(back):
        size = back.shape[1] // Y_CHIPS
        for i, ref in enumerate(back_refs):
            for j in range(Y_CHIPS):
                at = pl.multiple_of((high ^ j) * size, size)
                ref[:, pl.ds(at, size)] = back[i * rows : (i + 1) * rows, j * size : (j + 1) * size].astype(BF)

    @pl.when(step == 0)
    def _():
        send_ref[...] = part.astype(BF)
        store(dot(dvalues, theirs_ref[...], 1, 1))

    @pl.when(step == 1)
    def _():
        keep_ref[...] = part.astype(BF)
        store(dot(dvalues, mine_ref[...], 1, 1))


def weight_partials(where, tokens, columns, dvalues, mine, theirs):
    rows = tokens.shape[0]
    depth, width = mine.shape
    whole = pl.BlockSpec((depth, width), lambda step, where: (0, 0))
    part = pl.BlockSpec((rows, width), lambda step, where: (0, 0))
    own = pl.BlockSpec((rows, depth), lambda step, where: (0, where[0] * 2 + (1 - (where[1] ^ step))))
    other = pl.BlockSpec((rows, depth), lambda step, where: (0, 1 - (where[1] ^ step)))
    spec = pltpu.PrefetchScalarGridSpec(
        num_scalar_prefetch=1,
        grid=(2,),
        in_specs=[own] + [other] * 3 + [part] * 4 + [whole, whole],
        out_specs=[whole, whole] + [other] * 4,
    )
    return pl.pallas_call(
        weight_kernel,
        grid_spec=spec,
        out_shape=[jax.ShapeDtypeStruct((depth, width), BF)] * 2
        + [jax.ShapeDtypeStruct((rows, 2 * depth), BF)] * 4,
        compiler_params=pltpu.CompilerParams(dimension_semantics=("arbitrary",), vmem_limit_bytes=63 << 20),
        cost_estimate=lasting(5),
        name="weights",
    )(where, tokens, *columns, *dvalues, mine, theirs)


def place_kernel(where_ref, t0_ref, t1_ref, t2_ref, t3_ref, out_ref):
    width = t0_ref.shape[1]
    for i, ref in enumerate((t0_ref, t1_ref, t2_ref, t3_ref)):
        at = pl.multiple_of((where_ref[0] ^ i) * width, width)
        out_ref[:, pl.ds(at, width)] = ref[...]


def placed(where, pieces):
    rows, width = pieces[0].shape
    return pl.pallas_call(
        place_kernel,
        in_specs=[pl.BlockSpec(memory_space=pltpu.SMEM)] + [pl.BlockSpec(memory_space=pltpu.VMEM)] * 4,
        out_specs=pl.BlockSpec(memory_space=pltpu.VMEM),
        out_shape=jax.ShapeDtypeStruct((rows, X_CHIPS * width), BF),
        cost_estimate=lasting(2.4),
        name="place",
    )(where, *pieces)


def after(earlier, *later):
    return lax.optimization_barrier((later, earlier))[0]


def shards(queries, keys, tokens, value_matrix, output_gradient, segment_lengths, segment_offsets):
    rows = queries.shape[0]
    place = lax.axis_index("context")
    dp = lax.axis_index("dp")
    contexts = lax.axis_size("context")
    where = jnp.stack([dp // 2, dp % 2, place]).astype(jnp.int32)
    bias = visible_bias(place * rows, rows, segment_lengths[0], segment_offsets[0])

    rings = contexts // Y_CHIPS
    along_z = [[y * rings + z for z in range(rings)] for y in range(Y_CHIPS)]
    copies = jnp.broadcast_to(value_matrix[None], (rings,) + value_matrix.shape)
    ring = lax.all_to_all(copies, "context", 0, 0, axis_index_groups=along_z, tiled=True)
    (moving_tokens,) = after(copies, tokens)
    sent = column_blocks(where, moving_tokens)
    columns = [swapped(sent[i - 1], "dp", 2 * i) for i in (1, 2, 3)]
    ring = ring.reshape(rings * value_matrix.shape[0], value_matrix.shape[1])
    mine = jnp.concatenate([ring] + [swapped(ring, "context", rings * i) for i in (1, 2, 3)], axis=0)
    theirs = swapped(mine, "dp", 1)
    (moving_keys,) = after(sent, keys)
    k_even, unused, k_odd = neighbours(moving_keys)
    k = (k_even, keys, k_odd)
    (bias,) = after((columns[:2], ring), bias)

    dv_even, dv_own, dv_odd, lse = attention_probs(where, queries, k, output_gradient, bias)
    dv_even, dv_odd = after((columns, mine), dv_even, dv_odd)
    dvalues = collected(dv_even, dv_own, dv_odd)
    all_dvalues = [dvalues] + [swapped(dvalues, "dp", 2 * i) for i in (1, 2, 3)]

    groups = [[2 * x + core for x in range(X_CHIPS)] for core in range(2)]
    started = projected(where, tokens, columns, mine, theirs)
    parts = lax.all_to_all(started, "dp", 0, 0, axis_index_groups=groups, tiled=True)
    values = jnp.sum(parts.astype(F32), axis=0).astype(BF)
    v = neighbours(values)

    all_dvalues = after(started, *all_dvalues)
    send, keep, *back = weight_partials(where, tokens, columns, all_dvalues, mine, theirs)
    share = (keep.astype(F32) + swapped(send, "dp", 1).astype(F32)).astype(BF)
    share = share.reshape(contexts, -1, share.shape[1])
    share = lax.all_to_all(share, "context", 0, 0, tiled=True)
    dweight = jnp.sum(share.astype(F32), axis=0)
    back = [back[0]] + [swapped(back[i], "dp", 2 * i) for i in (1, 2, 3)]
    dtokens = placed(where, back)

    v = after(send, *v)
    dqueries, dk_even, dk_own, dk_odd = attention_scores(where, queries, k, v, output_gradient, bias, lse)
    dkeys = collected(dk_even, dk_own, dk_odd)
    return (dqueries, dkeys, dtokens, dweight)


def solution(mesh):
    both = P(("dp", "context"), None)
    in_specs = (both, both, both, both, both, P("dp", None), P("dp", None))
    out_specs = (both, both, both, both)
    return jax.shard_map(shards, mesh=mesh, in_specs=in_specs, out_specs=out_specs, check_vma=False)
```
